32 devices in a mesh: lat: 8 (over z, y), lon: 2 (over x), comp: 2 (over core).
Axes of the slice: x: 2, y: 2, z: 4, core: 2. Of those that a mesh axis runs over, the one named last changes fastest.
Arguments:
- atm_state: bfloat16 [192, 256, 384], P('lat', ('lon', 'comp')), may hold values from -6 to 6
- ocean_state: bfloat16 [192, 256, 256], P(('lat', 'comp'), 'lon'), may hold values from -6 to 6
- wet_mask: int32 [192, 256], P(('lat', 'comp'), 'lon'), may hold values 0 or 1
- legendre: bfloat16 [512, 384, 192], P(('lat', 'lon', 'comp')), may hold values from -4 to 4
- quad_weight: float32 [192], replicated, may hold values from 0.5 to 2
- spec_real: bfloat16 [384, 384], replicated, may hold values from -0.3125 to 0.3125
- spec_imag: bfloat16 [384, 384], replicated, may hold values from -0.3125 to 0.3125
- degree_gain: float32 [384], replicated, may hold values from 0.5 to 2
- atm_gain: float32 [2, 384], replicated, may hold values from 0.1 to 1.9
- atm_up: bfloat16 [384, 768], replicated, may hold values from -0.3125 to 0.3125
- atm_down: bfloat16 [768, 384], replicated, may hold values from -0.21875 to 0.21875
- atm_to_surface: bfloat16 [384, 32], replicated, may hold values from -0.3125 to 0.3125
- surface_to_atm: bfloat16 [32, 384], replicated, may hold values from -1 to 1
- ocean_to_surface: bfloat16 [256, 32], replicated, may hold values from -0.375 to 0.375
- surface_to_ocean: bfloat16 [32, 256], replicated, may hold values from -1 to 1
- ocean_kernel: bfloat16 [2, 7, 7, 256], replicated, may hold values from -0.875 to 0.875
- ocean_gain: float32 [2, 256], replicated, may hold values from 0.1 to 1.9
- ocean_up: bfloat16 [2, 256, 1024], replicated, may hold values from -0.375 to 0.375
- ocean_down: bfloat16 [2, 1024, 256], replicated, may hold values from -0.1875 to 0.1875
Outputs:
- atm_out: bfloat16 [192, 256, 384], P('lat', ('lon', 'comp'))
- ocean_out: bfloat16 [192, 256, 256], P(('lat', 'comp'), 'lon')
The draws below stay inside these ranges and needn't reach their ends.
All inputs are finite; a program needn't handle non-finite values. No bound on the sum of `wet_mask` on one device may be relied on, other than what follows from the above.
Results may differ from the reference program's by a relative error of at most 0.01.
Values may be sent and summed in bfloat16 or wider, within the bound.
A program may use at most 128 MiB of HBM per device.

```python
import math
import jax
import jax.numpy as jnp
from jax import lax

C = 384
HID = 768
OC = 256
OHID = 1024
SURF = 32
MODES = 512
DEG = 384
STENCIL_TAPS = 7
OCEAN_DILATION = 2
LAT_DEV = 24
NLAT = 192
NLON = 256
MODES_DEV = 16
N_LAT = 8
DEVICES = 32


def with_ends(entries, own_key, smallest, high):
    shape = entries.shape
    place = [jax.random.randint(jax.random.fold_in(own_key, axis), (), 0, shape[axis]) for axis in range(len(shape))]
    entries = entries.at[tuple(place)].set(smallest)
    longest = shape.index(max(shape))
    place[longest] = (place[longest] + 1) % shape[longest]
    return entries.at[tuple(place)].set(high)


def level_of(own_key, shape, cuts, least, high):
    level = 1.0
    for axis_at, parts in cuts:
        steps = jax.random.uniform(jax.random.fold_in(jax.random.fold_in(own_key, 6), axis_at), (parts,), jnp.float32, least / len(cuts), high / len(cuts))
        level = level * jnp.repeat(jnp.exp(steps), shape[axis_at] // parts).reshape((-1,) + (1,) * (len(shape) - 1 - axis_at))
    return level


def noise(rng, shape, scale, reach, split=(), kind=jnp.bfloat16):
    values = scale * jax.random.normal(rng, shape, jnp.float32)
    if split:
        values = values * level_of(rng, shape, split, -0.22, 0.18)
    return jnp.clip(values, -reach, reach).astype(kind)


def setup_inputs(seed: int = 0) -> dict:
    arg_keys = jax.random.split(jax.random.key(seed), 20)
    return {
        "atm_state": noise(arg_keys[0], (NLAT, NLON, C), 1.0, 6.0, ((0, 8), (1, 4))),
        "ocean_state": noise(arg_keys[1], (NLAT, NLON, OC), 1.0, 6.0, ((0, 16), (1, 2))),
        "wet_mask": with_ends((jax.random.randint(arg_keys[2], (NLAT, NLON), 0, 3) < 2).astype(jnp.int32), jax.random.fold_in(arg_keys[2], 1), 0, 1),
        "legendre": noise(arg_keys[3], (MODES, DEG, NLAT), 1.0, 4.0, ((0, 32),)),
        "quad_weight": jnp.clip(jnp.exp(jax.random.uniform(arg_keys[4], (NLAT,), jnp.float32, math.log(0.5), math.log(2.0))), 0.5, 2.0),
        "spec_real": noise(arg_keys[5], (C, C), C ** -0.5, 0.3125),
        "spec_imag": noise(arg_keys[6], (C, C), C ** -0.5, 0.3125),
        "degree_gain": jnp.clip(jnp.exp(jax.random.uniform(arg_keys[7], (DEG,), jnp.float32, math.log(0.5), math.log(2.0))), 0.5, 2.0),
        "atm_gain": jnp.clip(1.0 + 0.18 * jax.random.normal(arg_keys[8], (2, C), jnp.float32), 0.1, 1.9),
        "atm_up": noise(arg_keys[9], (C, HID), C ** -0.5, 0.3125),
        "atm_down": noise(arg_keys[10], (HID, C), HID ** -0.5, 0.21875),
        "atm_to_surface": noise(arg_keys[11], (C, SURF), C ** -0.5, 0.3125),
        "surface_to_atm": noise(arg_keys[12], (SURF, C), SURF ** -0.5, 1.0),
        "ocean_to_surface": noise(arg_keys[13], (OC, SURF), OC ** -0.5, 0.375),
        "surface_to_ocean": noise(arg_keys[14], (SURF, OC), SURF ** -0.5, 1.0),
        "ocean_kernel": noise(arg_keys[15], (2, STENCIL_TAPS, STENCIL_TAPS, OC), (STENCIL_TAPS * STENCIL_TAPS) ** -0.5, 0.875),
        "ocean_gain": jnp.clip(1.0 + 0.18 * jax.random.normal(arg_keys[16], (2, OC), jnp.float32), 0.1, 1.9),
        "ocean_up": noise(arg_keys[17], (2, OC, OHID), OC ** -0.5, 0.375),
        "ocean_down": noise(arg_keys[18], (2, OHID, OC), OHID ** -0.5, 0.1875),
    }


epsilon = 1e-05

def layer_norm(values, gain):
    centred = values - lax.optimization_barrier(jnp.mean(values, axis=-1, keepdims=True))
    spread = lax.optimization_barrier(jnp.mean(centred * centred, axis=-1, keepdims=True))
    return centred * lax.rsqrt(spread + epsilon) * gain

def wave_table(row_index, circle):
    longitude = jnp.arange(circle, dtype=jnp.int32)
    wavenumber = row_index // 2
    phases = wavenumber[:, None] * longitude[None, :] % circle
    angles = phases.astype(jnp.float32) * (2.0 * math.pi / circle)
    waves = jnp.where((row_index % 2 == 0)[:, None], jnp.cos(angles), -jnp.sin(angles))
    return (wavenumber, waves)

def forward_table(row_index, circle):
    wavenumber, waves = wave_table(row_index, circle)
    return (waves.T / math.sqrt(circle)).astype(jnp.bfloat16)

def inverse_table(row_index, circle):
    wavenumber, waves = wave_table(row_index, circle)
    factor = jnp.where(wavenumber == 0, 1.0, 2.0).astype(jnp.float32)
    return (waves * factor[:, None] / math.sqrt(circle)).astype(jnp.bfloat16)

def spectral_filter(gathered, table, quad_weight, spec_real, spec_imag, degree_gain):
    count = table.shape[0]
    lat_total = table.shape[2]
    channels = gathered.shape[2]
    split_parts = gathered.reshape(lat_total, count, 2, channels)
    weighted = (table.astype(jnp.float32) * (quad_weight / lat_total)).astype(jnp.bfloat16)
    coeffs = jnp.einsum('mln,nmpc->mplc', weighted.astype(jnp.float32), split_parts.astype(jnp.float32)).astype(jnp.bfloat16)
    real_part = coeffs[:, 0]
    imag_part = coeffs[:, 1]
    mixed_real = jnp.dot(real_part, spec_real, preferred_element_type=jnp.float32) - jnp.dot(imag_part, spec_imag, preferred_element_type=jnp.float32)
    mixed_imag = jnp.dot(real_part, spec_imag, preferred_element_type=jnp.float32) + jnp.dot(imag_part, spec_real, preferred_element_type=jnp.float32)
    scaled = (jnp.stack([mixed_real, mixed_imag], axis=1) * degree_gain[:, None]).astype(jnp.bfloat16)
    returned = jnp.einsum('mln,mplc->nmpc', table.astype(jnp.float32), scaled.astype(jnp.float32)).astype(jnp.bfloat16)
    return returned.reshape(lat_total, 2 * count, channels)

def ocean_block(padded_field, kernel, gain, up_weight, down_weight):
    stencil_reach = STENCIL_TAPS // 2 * OCEAN_DILATION
    tile_height = padded_field.shape[0] - 2 * stencil_reach
    tile_breadth = padded_field.shape[1] - 2 * stencil_reach
    stencil = jnp.zeros((tile_height, tile_breadth, padded_field.shape[2]), jnp.float32)
    for row_offset_tap in range(STENCIL_TAPS):
        for column_tap in range(STENCIL_TAPS):
            stencil_window = padded_field[row_offset_tap * OCEAN_DILATION:row_offset_tap * OCEAN_DILATION + tile_height, column_tap * OCEAN_DILATION:column_tap * OCEAN_DILATION + tile_breadth]
            stencil = stencil + stencil_window.astype(jnp.float32) * kernel[row_offset_tap, column_tap].astype(jnp.float32)
    normed = layer_norm(stencil, gain).astype(jnp.bfloat16)
    hidden = jax.nn.gelu(jnp.dot(normed, up_weight, preferred_element_type=jnp.float32)).astype(jnp.bfloat16)
    centre = padded_field[stencil_reach:stencil_reach + tile_height, stencil_reach:stencil_reach + tile_breadth]
    return (centre.astype(jnp.float32) + jnp.dot(hidden, down_weight, preferred_element_type=jnp.float32)).astype(jnp.bfloat16)

def ocean_layer(state, kernel, gain, up_weight, down_weight):
    stencil_reach = STENCIL_TAPS // 2 * OCEAN_DILATION
    padded_field = jnp.pad(state, ((stencil_reach, stencil_reach), (stencil_reach, stencil_reach), (0, 0)))

    def one_band(band_index):
        start = (band_index * LAT_DEV).astype(jnp.int32)
        piece = lax.dynamic_slice_in_dim(padded_field, start, LAT_DEV + 2 * stencil_reach, 0)
        return ocean_block(piece, kernel, gain, up_weight, down_weight)
    bands = lax.map(one_band, jnp.arange(N_LAT, dtype=jnp.int32))
    return bands.reshape(NLAT, NLON, OC)

def reference(atm_state, ocean_state, wet_mask, legendre, quad_weight, spec_real, spec_imag, degree_gain, atm_gain, atm_up, atm_down, atm_to_surface, surface_to_atm, ocean_to_surface, surface_to_ocean, ocean_kernel, ocean_gain, ocean_up, ocean_down):
    wet = wet_mask.astype(jnp.float32)[:, :, None]
    ocean_flux = (jnp.dot(ocean_state, ocean_to_surface, preferred_element_type=jnp.float32) * wet).astype(jnp.bfloat16)
    forced = atm_state.astype(jnp.float32) + jnp.dot(ocean_flux, surface_to_atm, preferred_element_type=jnp.float32)
    normed = layer_norm(forced, atm_gain[0]).astype(jnp.bfloat16)
    row_index = jnp.arange(2 * MODES, dtype=jnp.int32)
    forward = forward_table(row_index, NLON)
    inverse = inverse_table(row_index, NLON)

    def to_spectrum(lat_band):
        return jnp.einsum('anc,nr->arc', lat_band.astype(jnp.float32), forward.astype(jnp.float32)).astype(jnp.bfloat16)
    spectrum = lax.map(to_spectrum, normed.reshape(N_LAT, LAT_DEV, NLON, C))
    spectrum = spectrum.reshape(NLAT, DEVICES, 2 * MODES_DEV, C)
    owner_blocks = jnp.moveaxis(spectrum, 1, 0)
    table_blocks = legendre.reshape(DEVICES, MODES_DEV, DEG, NLAT)

    def one_owner(pieces):
        return spectral_filter(pieces[0], pieces[1], quad_weight, spec_real, spec_imag, degree_gain)
    filtered = lax.map(one_owner, (owner_blocks, table_blocks))
    returned = jnp.moveaxis(filtered, 0, 1).reshape(N_LAT, LAT_DEV, 2 * MODES, C)

    def finish(pieces):
        lat_band, forced_band = pieces
        spatial = jnp.einsum('arc,rn->anc', lat_band.astype(jnp.float32), inverse.astype(jnp.float32)).astype(jnp.bfloat16)
        mixed = forced_band + spatial.astype(jnp.float32)
        normed_two = layer_norm(mixed, atm_gain[1]).astype(jnp.bfloat16)
        hidden = jax.nn.gelu(jnp.dot(normed_two, atm_up, preferred_element_type=jnp.float32)).astype(jnp.bfloat16)
        return (mixed + jnp.dot(hidden, atm_down, preferred_element_type=jnp.float32)).astype(jnp.bfloat16)
    atm_out = lax.map(finish, (returned, forced.reshape(N_LAT, LAT_DEV, NLON, C))).reshape(NLAT, NLON, C)
    atm_flux = jnp.dot(atm_state, atm_to_surface, preferred_element_type=jnp.float32).astype(jnp.bfloat16)
    current = (ocean_state.astype(jnp.float32) + wet * jnp.dot(atm_flux, surface_to_ocean, preferred_element_type=jnp.float32)).astype(jnp.bfloat16)
    for block_index in range(2):
        current = ocean_layer(current, ocean_kernel[block_index], ocean_gain[block_index], ocean_up[block_index], ocean_down[block_index])
    ocean_out = jnp.where(wet_mask[:, :, None] == 1, current, ocean_state)
    return (atm_out, ocean_out)
```

```python
import math

import jax
import jax.numpy as jnp
from jax import lax
from jax.sharding import PartitionSpec as P

MODES = 512
STENCIL_TAPS = 7
OCEAN_DILATION = 2
COLUMNS = ("lon", "comp")
EVERY = ("lat", "lon", "comp")


epsilon = 1e-05


def padded(block, sides, width):
    for axis, dim in sides:
        count = lax.axis_size(axis)
        forward = [(i, i + 1) for i in range(count - 1)]
        backward = [(target, source) for source, target in forward]
        low = lax.ppermute(
            lax.slice_in_dim(block, block.shape[dim] - width, None, axis=dim), axis, forward
        )
        high = lax.ppermute(lax.slice_in_dim(block, 0, width, axis=dim), axis, backward)
        block = jnp.concatenate([low, block, high], axis=dim)
    return block


def layer_norm(values, gain):
    centred = values - jnp.mean(values, axis=-1, keepdims=True)
    spread = jnp.mean(centred * centred, axis=-1, keepdims=True)
    return centred * lax.rsqrt(spread + epsilon) * gain


def wave_table(row_index, circle):
    longitude = jnp.arange(circle, dtype=jnp.int32)
    wavenumber = row_index // 2
    phases = wavenumber[:, None] * longitude[None, :] % circle
    angles = phases.astype(jnp.float32) * (2.0 * math.pi / circle)
    waves = jnp.where((row_index % 2 == 0)[:, None], jnp.cos(angles), -jnp.sin(angles))
    return (wavenumber, waves)


def forward_table(row_index, circle):
    wavenumber, waves = wave_table(row_index, circle)
    return (waves.T / math.sqrt(circle)).astype(jnp.bfloat16)


def inverse_table(row_index, circle):
    wavenumber, waves = wave_table(row_index, circle)
    factor = jnp.where(wavenumber == 0, 1.0, 2.0).astype(jnp.float32)
    return (waves * factor[:, None] / math.sqrt(circle)).astype(jnp.bfloat16)


def reorder_rows(total_rows, owned, lat_count, col_count):
    positions = jnp.arange(total_rows, dtype=jnp.int32)
    stride = lat_count * owned
    return (
        owned * (positions % stride // owned * col_count + positions // stride) + positions % owned
    )


def spectral_filter(gathered, table, quad_weight, spec_real, spec_imag, degree_gain):
    count = table.shape[0]
    lat_total = table.shape[2]
    channels = gathered.shape[2]
    split_parts = gathered.reshape(lat_total, count, 2, channels)
    weighted = (table.astype(jnp.float32) * (quad_weight / lat_total)).astype(jnp.bfloat16)
    coeffs = jnp.einsum(
        "mln,nmpc->mplc", weighted, split_parts, preferred_element_type=jnp.float32
    ).astype(jnp.bfloat16)
    real_part = coeffs[:, 0]
    imag_part = coeffs[:, 1]
    mixed_real = jnp.dot(real_part, spec_real, preferred_element_type=jnp.float32) - jnp.dot(
        imag_part, spec_imag, preferred_element_type=jnp.float32
    )
    mixed_imag = jnp.dot(real_part, spec_imag, preferred_element_type=jnp.float32) + jnp.dot(
        imag_part, spec_real, preferred_element_type=jnp.float32
    )
    scaled = (jnp.stack([mixed_real, mixed_imag], axis=1) * degree_gain[:, None]).astype(
        jnp.bfloat16
    )
    returned = jnp.einsum(
        "mln,mplc->nmpc", table, scaled, preferred_element_type=jnp.float32
    ).astype(jnp.bfloat16)
    return returned.reshape(lat_total, 2 * count, channels)


def folds(circle, lat_dev, col_count, devices):
    return (
        MODES == 2 * circle
        and lat_dev % col_count == 0
        and devices % 4 == 0
        and (circle // 2) % devices == 0
        and (MODES // devices) % 4 == 0
    )


def folded_waves(circle):
    longitude = jnp.arange(circle, dtype=jnp.int32)
    row_index = jnp.arange(circle, dtype=jnp.int32)
    wavenumber = jnp.where(row_index == 1, circle // 2, row_index // 2)
    phases = wavenumber[:, None] * longitude[None, :] % circle
    angles = phases.astype(jnp.float32) * (2.0 * math.pi / circle)
    cosine = ((row_index % 2 == 0) | (row_index == 1))[:, None]
    return jnp.where(cosine, jnp.cos(angles), -jnp.sin(angles)) / math.sqrt(circle)


def folded_operators(table, quad_weight, degree_gain):
    devices = lax.axis_size(EVERY)
    me = lax.axis_index(EVERY)
    count, degrees, lat_total = table.shape
    group = devices // 4
    part = count // 4
    family = me // group
    scaled = (table.astype(jnp.float32) * degree_gain[:, None]).astype(jnp.bfloat16)
    operators = jnp.einsum("mlt,mlu->mtu", table, scaled, preferred_element_type=jnp.float32)
    operators = operators * (quad_weight / lat_total)
    first_scale = jnp.where(me == 0, 0.5, 1.0).astype(jnp.float32)
    scales = jnp.where(jnp.arange(count) == 0, first_scale, 1.0)
    operators = (operators * scales[:, None, None]).astype(jnp.bfloat16)
    turn = []
    for base in (group, 3 * group):
        for i in range(group):
            turn.append((base + (i + 1) % group, base + i))
    rotated = lax.ppermute(operators[:1], EVERY, turn)
    mirrored = jnp.concatenate([rotated, jnp.flip(operators[1:], axis=0)], axis=0)
    ordered = jnp.where(family % 2 == 1, mirrored, operators)
    received = []
    for step in range(4):
        pairs = []
        for source in range(devices):
            kind, place = source // group, source % group
            place = group - 1 - place if kind % 2 else place
            pairs.append((source, 4 * place + (step + kind) % 4))
        piece = lax.dynamic_slice_in_dim(ordered, (step + family) % 4 * part, part, axis=0)
        received.append(lax.ppermute(piece, EVERY, pairs).astype(jnp.float32))
    even = received[0] + received[2]
    odd = received[1] + received[3]
    direct = jnp.where(me % 2 == 0, even, odd)
    mirror = jnp.where(me % 2 == 0, odd, even)
    lone = ((me == 0) & (jnp.arange(part) == 0))[:, None, None]
    both = direct + mirror
    gap = jnp.where(lone, 0.0, direct - mirror)
    top = jnp.concatenate([jnp.where(lone, direct, both), -gap], axis=2)
    bottom = jnp.concatenate([gap, jnp.where(lone, mirror, both)], axis=2)
    return (2.0 * top).astype(jnp.bfloat16), (2.0 * bottom).astype(jnp.bfloat16)


def folded_spectral(normed, legendre, quad_weight, spec_real, spec_imag, degree_gain, circle):
    width = normed.shape[2]
    top, bottom = folded_operators(legendre, quad_weight, degree_gain)
    slots = top.shape[0]
    waves = folded_waves(circle).astype(jnp.bfloat16)
    columns = lax.all_to_all(normed, COLUMNS, split_axis=0, concat_axis=1, tiled=True)
    spectrum = jnp.einsum(
        "rn,tnc->trc", waves, columns, preferred_element_type=jnp.float32
    ).astype(jnp.bfloat16)
    gathered = lax.all_to_all(spectrum, EVERY, split_axis=1, concat_axis=0, tiled=True)
    lat_total = gathered.shape[0]
    channels = jnp.concatenate([spec_real, spec_imag], axis=1)
    turned = gathered.reshape(lat_total, slots, 2, width).transpose(1, 2, 0, 3)
    mixed = jnp.dot(turned, channels, preferred_element_type=jnp.float32).astype(jnp.bfloat16)
    upper = jnp.concatenate([mixed[:, 0, :, :width], mixed[:, 1, :, width:]], axis=1)
    lower = jnp.concatenate([mixed[:, 0, :, width:], mixed[:, 1, :, :width]], axis=1)
    cosine = jnp.einsum("stu,suc->stc", top, upper, preferred_element_type=jnp.float32)
    sine = jnp.einsum("stu,suc->stc", bottom, lower, preferred_element_type=jnp.float32)
    filtered = jnp.stack([cosine, sine], axis=1).astype(jnp.bfloat16)
    filtered = filtered.reshape(2 * slots, lat_total, width).transpose(1, 0, 2)
    returned = lax.all_to_all(filtered, EVERY, split_axis=0, concat_axis=1, tiled=True)
    spatial = jnp.einsum(
        "rn,trc->tnc", waves, returned, preferred_element_type=jnp.float32
    ).astype(jnp.bfloat16)
    return lax.all_to_all(spatial, COLUMNS, split_axis=1, concat_axis=0, tiled=True)


def plain_spectral(normed, legendre, quad_weight, spec_real, spec_imag, degree_gain, circle):
    lat_count = lax.axis_size("lat")
    col_count = lax.axis_size(("lon", "comp"))
    total_rows = 2 * MODES
    owned = 2 * legendre.shape[0]
    natural = jnp.arange(total_rows, dtype=jnp.int32)
    columns = lax.all_to_all(normed, ("lon", "comp"), split_axis=2, concat_axis=1, tiled=True)
    forward = forward_table(natural, circle)
    inverse = inverse_table(reorder_rows(total_rows, owned, lat_count, col_count), circle)
    spectrum = jnp.einsum(
        "anc,nr->arc", columns, forward, preferred_element_type=jnp.float32
    ).astype(jnp.bfloat16)
    gathered = lax.all_to_all(
        lax.all_to_all(spectrum, "lat", split_axis=1, concat_axis=0, tiled=True),
        ("lon", "comp"),
        split_axis=1,
        concat_axis=2,
        tiled=True,
    )
    filtered = spectral_filter(gathered, legendre, quad_weight, spec_real, spec_imag, degree_gain)
    returned = lax.all_to_all(
        lax.all_to_all(filtered, "lat", split_axis=0, concat_axis=1, tiled=True),
        ("lon", "comp"),
        split_axis=2,
        concat_axis=1,
        tiled=True,
    )
    spatial = jnp.einsum(
        "arc,rn->anc", returned, inverse, preferred_element_type=jnp.float32
    ).astype(jnp.bfloat16)
    return lax.all_to_all(spatial, ("lon", "comp"), split_axis=1, concat_axis=2, tiled=True)


def ocean_block(padded_field, kernel, gain, up_weight, down_weight):
    stencil_reach = STENCIL_TAPS // 2 * OCEAN_DILATION
    tile_height = padded_field.shape[0] - 2 * stencil_reach
    tile_breadth = padded_field.shape[1] - 2 * stencil_reach
    stencil = jnp.zeros((tile_height, tile_breadth, padded_field.shape[2]), jnp.float32)
    for row_offset_tap in range(STENCIL_TAPS):
        for column_tap in range(STENCIL_TAPS):
            stencil_window = padded_field[
                row_offset_tap * OCEAN_DILATION : row_offset_tap * OCEAN_DILATION + tile_height,
                column_tap * OCEAN_DILATION : column_tap * OCEAN_DILATION + tile_breadth,
            ]
            stencil = stencil + stencil_window.astype(jnp.float32) * kernel[
                row_offset_tap, column_tap
            ].astype(jnp.float32)
    normed = layer_norm(stencil, gain).astype(jnp.bfloat16)
    hidden = jax.nn.gelu(jnp.dot(normed, up_weight, preferred_element_type=jnp.float32)).astype(
        jnp.bfloat16
    )
    centre = padded_field[
        stencil_reach : stencil_reach + tile_height, stencil_reach : stencil_reach + tile_breadth
    ]
    return (
        centre.astype(jnp.float32)
        + jnp.dot(hidden, down_weight, preferred_element_type=jnp.float32)
    ).astype(jnp.bfloat16)


def local(
    atm_state,
    ocean_state,
    wet_mask,
    legendre,
    quad_weight,
    spec_real,
    spec_imag,
    degree_gain,
    atm_gain,
    atm_up,
    atm_down,
    atm_to_surface,
    surface_to_atm,
    ocean_to_surface,
    surface_to_ocean,
    ocean_kernel,
    ocean_gain,
    ocean_up,
    ocean_down,
):
    col_count = lax.axis_size(COLUMNS)
    lat_dev, lon_dev, width = atm_state.shape
    circle = lon_dev * col_count
    wet = wet_mask.astype(jnp.float32)[:, :, None]
    ocean_flux = (
        jnp.dot(ocean_state, ocean_to_surface, preferred_element_type=jnp.float32) * wet
    ).astype(jnp.bfloat16)
    atm_flux = jnp.dot(atm_state, atm_to_surface, preferred_element_type=jnp.float32).astype(
        jnp.bfloat16
    )
    flux_here = lax.all_to_all(ocean_flux, "comp", split_axis=1, concat_axis=0, tiled=True)
    flux_sea = lax.all_to_all(atm_flux, "comp", split_axis=0, concat_axis=1, tiled=True)
    forced = atm_state.astype(jnp.float32) + jnp.dot(
        flux_here, surface_to_atm, preferred_element_type=jnp.float32
    )
    normed = layer_norm(forced, atm_gain[0]).astype(jnp.bfloat16)
    run_spectral = (
        folded_spectral
        if folds(circle, lat_dev, col_count, lax.axis_size(EVERY))
        else plain_spectral
    )
    spectral = run_spectral(
        normed, legendre, quad_weight, spec_real, spec_imag, degree_gain, circle
    )
    mixed = forced + spectral.astype(jnp.float32)
    normed_two = layer_norm(mixed, atm_gain[1]).astype(jnp.bfloat16)
    hidden = jax.nn.gelu(jnp.dot(normed_two, atm_up, preferred_element_type=jnp.float32)).astype(
        jnp.bfloat16
    )
    atm_out = (mixed + jnp.dot(hidden, atm_down, preferred_element_type=jnp.float32)).astype(
        jnp.bfloat16
    )
    ocean_in = (
        ocean_state.astype(jnp.float32)
        + wet * jnp.dot(flux_sea, surface_to_ocean, preferred_element_type=jnp.float32)
    ).astype(jnp.bfloat16)
    stencil_reach = STENCIL_TAPS // 2 * OCEAN_DILATION
    sides = ((("lat", "comp"), 0), ("lon", 1))
    current = ocean_in
    for k in range(2):
        field = padded(current, sides, stencil_reach)
        current = ocean_block(field, ocean_kernel[k], ocean_gain[k], ocean_up[k], ocean_down[k])
    ocean_out = jnp.where(wet_mask[:, :, None] == 1, current, ocean_state)
    return (atm_out, ocean_out)


def solution(mesh):
    placed = (
        P("lat", ("lon", "comp"), None),
        P(("lat", "comp"), "lon", None),
        P(("lat", "comp"), "lon"),
        P(("lat", "lon", "comp"), None, None),
        P(),
        P(),
        P(),
        P(),
        P(),
        P(),
        P(),
        P(),
        P(),
        P(),
        P(),
        P(),
        P(),
        P(),
        P(),
    )
    return jax.shard_map(
        local,
        mesh=mesh,
        in_specs=placed,
        out_specs=(P("lat", ("lon", "comp"), None), P(("lat", "comp"), "lon", None)),
        check_vma=False,
    )
```

```python
import math

import jax
import jax.numpy as jnp
from jax import lax
from jax.experimental import pallas as pl
from jax.experimental.pallas import tpu as pltpu
from jax.sharding import PartitionSpec as P

MODES = 512
STENCIL_TAPS = 7
OCEAN_DILATION = 2
COLUMNS = ("lon", "comp")
EVERY = ("lat", "lon", "comp")


epsilon = 1e-05


def padded(block, sides, width):
    for axis, dim in sides:
        count = lax.axis_size(axis)
        forward = [(i, i + 1) for i in range(count - 1)]
        backward = [(target, source) for source, target in forward]
        low = lax.ppermute(
            lax.slice_in_dim(block, block.shape[dim] - width, None, axis=dim), axis, forward
        )
        high = lax.ppermute(lax.slice_in_dim(block, 0, width, axis=dim), axis, backward)
        block = jnp.concatenate([low, block, high], axis=dim)
    return block


def layer_norm(values, gain):
    centred = values - jnp.mean(values, axis=-1, keepdims=True)
    spread = jnp.mean(centred * centred, axis=-1, keepdims=True)
    return centred * lax.rsqrt(spread + epsilon) * gain


def wave_table(row_index, circle):
    longitude = jnp.arange(circle, dtype=jnp.int32)
    wavenumber = row_index // 2
    phases = wavenumber[:, None] * longitude[None, :] % circle
    angles = phases.astype(jnp.float32) * (2.0 * math.pi / circle)
    waves = jnp.where((row_index % 2 == 0)[:, None], jnp.cos(angles), -jnp.sin(angles))
    return (wavenumber, waves)


def forward_table(row_index, circle):
    _, waves = wave_table(row_index, circle)
    return (waves.T / math.sqrt(circle)).astype(jnp.bfloat16)


def inverse_table(row_index, circle):
    wavenumber, waves = wave_table(row_index, circle)
    factor = jnp.where(wavenumber == 0, 1.0, 2.0).astype(jnp.float32)
    return (waves * factor[:, None] / math.sqrt(circle)).astype(jnp.bfloat16)


def reorder_rows(total_rows, owned, lat_count, col_count):
    positions = jnp.arange(total_rows, dtype=jnp.int32)
    stride = lat_count * owned
    return (
        owned * (positions % stride // owned * col_count + positions // stride) + positions % owned
    )


def spectral_filter(gathered, table, quad_weight, spec_real, spec_imag, degree_gain):
    count = table.shape[0]
    lat_total = table.shape[2]
    channels = gathered.shape[2]
    split_parts = gathered.reshape(lat_total, count, 2, channels)
    weighted = (table.astype(jnp.float32) * (quad_weight / lat_total)).astype(jnp.bfloat16)
    coeffs = jnp.einsum(
        "mln,nmpc->mplc", weighted, split_parts, preferred_element_type=jnp.float32
    ).astype(jnp.bfloat16)
    real_part = coeffs[:, 0]
    imag_part = coeffs[:, 1]
    mixed_real = jnp.dot(real_part, spec_real, preferred_element_type=jnp.float32) - jnp.dot(
        imag_part, spec_imag, preferred_element_type=jnp.float32
    )
    mixed_imag = jnp.dot(real_part, spec_imag, preferred_element_type=jnp.float32) + jnp.dot(
        imag_part, spec_real, preferred_element_type=jnp.float32
    )
    scaled = (jnp.stack([mixed_real, mixed_imag], axis=1) * degree_gain[:, None]).astype(
        jnp.bfloat16
    )
    returned = jnp.einsum(
        "mln,mplc->nmpc", table, scaled, preferred_element_type=jnp.float32
    ).astype(jnp.bfloat16)
    return returned.reshape(lat_total, 2 * count, channels)


def folds(circle, lat_dev, col_count, devices):
    return (
        MODES == 2 * circle
        and lat_dev % col_count == 0
        and devices % 4 == 0
        and (circle // 2) % devices == 0
        and (MODES // devices) % 4 == 0
    )


def place_of(kind, i, group):
    return kind * group + (group - 1 - i if kind % 2 else i)


def folded_waves(circle, devices):
    longitude = jnp.arange(circle, dtype=jnp.int32)
    position = jnp.arange(circle, dtype=jnp.int32)
    group = devices // 4
    owned = circle // devices
    owner = position // owned
    kind, place = owner // group, owner % group
    place = jnp.where(kind % 2 == 1, group - 1 - place, place)
    row_index = (4 * place + kind) * owned + position % owned
    wavenumber = jnp.where(row_index == 1, circle // 2, row_index // 2)
    phases = wavenumber[:, None] * longitude[None, :] % circle
    angles = phases.astype(jnp.float32) * (2.0 * math.pi / circle)
    cosine = ((row_index % 2 == 0) | (row_index == 1))[:, None]
    return jnp.where(cosine, jnp.cos(angles), -jnp.sin(angles)) / math.sqrt(circle)


def folded_operators(table, quad_weight, degree_gain):
    devices = lax.axis_size(EVERY)
    me = lax.axis_index(EVERY)
    count, _, lat_total = table.shape
    group = devices // 4
    part = count // 4
    family = me // group
    scaled = (table.astype(jnp.float32) * degree_gain[:, None]).astype(jnp.bfloat16)
    operators = jnp.einsum(
        "mlt,mlu->mtu", table, scaled, preferred_element_type=jnp.float32
    )
    operators = operators * (quad_weight / lat_total)
    first_scale = jnp.where(me == 0, 0.5, 1.0).astype(jnp.float32)
    scales = jnp.where(jnp.arange(count) == 0, first_scale, 1.0)
    operators = (operators * scales[:, None, None]).astype(jnp.bfloat16)
    turn = []
    for base in (group, 3 * group):
        for i in range(group):
            turn.append((base + (i + 1) % group, base + i))
    rotated = lax.ppermute(operators[:1], EVERY, turn)
    mirrored = jnp.concatenate([rotated, jnp.flip(operators[1:], axis=0)], axis=0)
    ordered = jnp.where(family % 2 == 1, mirrored, operators)
    received = [lax.dynamic_slice_in_dim(ordered, family * part, part, axis=0)]
    for shift in range(1, 4):
        pairs = []
        for i in range(group):
            for kind in range(4):
                pairs.append((place_of(kind, i, group), place_of(kind ^ shift, i, group)))
        piece = lax.dynamic_slice_in_dim(ordered, (family ^ shift) * part, part, axis=0)
        received.append(lax.ppermute(piece, EVERY, pairs))
    received = [value.astype(jnp.float32) for value in received]
    same = received[0] + received[2]
    other = received[1] + received[3]
    direct = jnp.where(family % 2 == 0, same, other)
    mirror = jnp.where(family % 2 == 0, other, same)
    lone = ((me == 0) & (jnp.arange(part) == 0))[:, None, None]
    both = direct + mirror
    gap = jnp.where(lone, 0.0, direct - mirror)
    top = jnp.concatenate([jnp.where(lone, direct, both), -gap], axis=2)
    bottom = jnp.concatenate([gap, jnp.where(lone, mirror, both)], axis=2)
    return (2.0 * top).astype(jnp.bfloat16), (2.0 * bottom).astype(jnp.bfloat16)


def folded_spectral(normed, legendre, quad_weight, spec_real, spec_imag, degree_gain, circle):
    width = normed.shape[2]
    top, bottom = folded_operators(legendre, quad_weight, degree_gain)
    slots = top.shape[0]
    waves = folded_waves(circle, lax.axis_size(EVERY)).astype(jnp.bfloat16)
    columns = lax.all_to_all(normed, COLUMNS, split_axis=0, concat_axis=1, tiled=True)
    spectrum = jnp.einsum(
        "rn,tnc->trc", waves, columns, preferred_element_type=jnp.float32
    ).astype(jnp.bfloat16)
    gathered = lax.all_to_all(spectrum, EVERY, split_axis=1, concat_axis=0, tiled=True)
    lat_total = gathered.shape[0]
    channels = jnp.concatenate([spec_real, spec_imag], axis=1)
    turned = gathered.reshape(lat_total, slots, 2, width).transpose(1, 2, 0, 3)
    mixed = jnp.dot(turned, channels, preferred_element_type=jnp.float32).astype(jnp.bfloat16)
    upper = jnp.concatenate([mixed[:, 0, :, :width], mixed[:, 1, :, width:]], axis=1)
    lower = jnp.concatenate([mixed[:, 0, :, width:], mixed[:, 1, :, :width]], axis=1)
    cosine = jnp.einsum("stu,suc->stc", top, upper, preferred_element_type=jnp.float32)
    sine = jnp.einsum("stu,suc->stc", bottom, lower, preferred_element_type=jnp.float32)
    filtered = jnp.stack([cosine, sine], axis=1).astype(jnp.bfloat16)
    filtered = filtered.reshape(2 * slots, lat_total, width).transpose(1, 0, 2)
    returned = lax.all_to_all(filtered, EVERY, split_axis=0, concat_axis=1, tiled=True)
    spatial = jnp.einsum(
        "rn,trc->tnc", waves, returned, preferred_element_type=jnp.float32
    ).astype(jnp.bfloat16)
    spectral = lax.all_to_all(spatial, COLUMNS, split_axis=1, concat_axis=0, tiled=True)
    return spectral, (spectrum, filtered)


def plain_spectral(normed, legendre, quad_weight, spec_real, spec_imag, degree_gain, circle):
    lat_count = lax.axis_size("lat")
    col_count = lax.axis_size(("lon", "comp"))
    total_rows = 2 * MODES
    owned = 2 * legendre.shape[0]
    natural = jnp.arange(total_rows, dtype=jnp.int32)
    columns = lax.all_to_all(normed, ("lon", "comp"), split_axis=2, concat_axis=1, tiled=True)
    forward = forward_table(natural, circle)
    inverse = inverse_table(reorder_rows(total_rows, owned, lat_count, col_count), circle)
    spectrum = jnp.einsum(
        "anc,nr->arc", columns, forward, preferred_element_type=jnp.float32
    ).astype(jnp.bfloat16)
    gathered = lax.all_to_all(
        lax.all_to_all(spectrum, "lat", split_axis=1, concat_axis=0, tiled=True),
        ("lon", "comp"),
        split_axis=1,
        concat_axis=2,
        tiled=True,
    )
    filtered = spectral_filter(gathered, legendre, quad_weight, spec_real, spec_imag, degree_gain)
    returned = lax.all_to_all(
        lax.all_to_all(filtered, "lat", split_axis=0, concat_axis=1, tiled=True),
        ("lon", "comp"),
        split_axis=2,
        concat_axis=1,
        tiled=True,
    )
    spatial = jnp.einsum(
        "arc,rn->anc", returned, inverse, preferred_element_type=jnp.float32
    ).astype(jnp.bfloat16)
    spectral = lax.all_to_all(spatial, COLUMNS, split_axis=1, concat_axis=2, tiled=True)
    return spectral, (spectrum, filtered)


def ocean_block(padded_field, kernel, gain, up_weight, down_weight):
    stencil_reach = STENCIL_TAPS // 2 * OCEAN_DILATION
    tile_height = padded_field.shape[0] - 2 * stencil_reach
    tile_breadth = padded_field.shape[1] - 2 * stencil_reach
    stencil = jnp.zeros((tile_height, tile_breadth, padded_field.shape[2]), jnp.float32)
    for row_offset_tap in range(STENCIL_TAPS):
        for column_tap in range(STENCIL_TAPS):
            stencil_window = padded_field[
                row_offset_tap * OCEAN_DILATION : row_offset_tap * OCEAN_DILATION + tile_height,
                column_tap * OCEAN_DILATION : column_tap * OCEAN_DILATION + tile_breadth,
            ]
            stencil = stencil + stencil_window.astype(jnp.float32) * kernel[
                row_offset_tap, column_tap
            ].astype(jnp.float32)
    normed = layer_norm(stencil, gain).astype(jnp.bfloat16)
    hidden = jax.nn.gelu(jnp.dot(normed, up_weight, preferred_element_type=jnp.float32)).astype(
        jnp.bfloat16
    )
    centre = padded_field[
        stencil_reach : stencil_reach + tile_height, stencil_reach : stencil_reach + tile_breadth
    ]
    return (
        centre.astype(jnp.float32)
        + jnp.dot(hidden, down_weight, preferred_element_type=jnp.float32)
    ).astype(jnp.bfloat16)


def ocean_kernel_body(
    field_ref, taps_ref, gain_ref, up_ref, down_ref, after_ref, out_ref, wide, normed
):
    rows, cols, width = out_ref.shape
    step = OCEAN_DILATION
    lanes = 128

    @pl.loop(0, rows + (STENCIL_TAPS - 1) * step)
    def _(row):
        wide[row] = field_ref[row].astype(jnp.float32)

    @pl.loop(0, rows // 2)
    def _(pair):
        base = pair // step * (2 * step) + pair % step
        for half in range(width // lanes):
            part = slice(half * lanes, (half + 1) * lanes)
            sums = [jnp.zeros((cols, lanes), jnp.float32) for _ in range(2)]
            for a in range(STENCIL_TAPS + 1):
                for b in range(STENCIL_TAPS):
                    window = wide[base + a * step, b * step : b * step + cols, part]
                    for which in range(2):
                        tap = a - which
                        if 0 <= tap < STENCIL_TAPS:
                            weight = taps_ref[tap * STENCIL_TAPS + b, :, part]
                            sums[which] = sums[which] + window * weight
            for which in range(2):
                normed[which * cols : (which + 1) * cols, part] = sums[which]
        stencil = normed[...]
        values = layer_norm(stencil, gain_ref[...]).astype(jnp.bfloat16)
        hidden = jax.nn.gelu(
            jnp.dot(values, up_ref[...], preferred_element_type=jnp.float32)
        ).astype(jnp.bfloat16)
        moved = jnp.dot(hidden, down_ref[...], preferred_element_type=jnp.float32)
        reach = STENCIL_TAPS // 2 * step
        for which in range(2):
            row = base + which * step
            centre = wide[row + reach, reach : reach + cols, :]
            out_ref[row] = (centre + moved[which * cols : (which + 1) * cols]).astype(
                out_ref.dtype
            )


def fast_ocean_block(field, kernel, gain, up_weight, down_weight, after):
    reach = STENCIL_TAPS // 2 * OCEAN_DILATION
    rows, cols, width = field.shape[0] - 2 * reach, field.shape[1] - 2 * reach, field.shape[2]
    hidden = up_weight.shape[1]
    taps = kernel.astype(jnp.float32).reshape(STENCIL_TAPS * STENCIL_TAPS, 1, width)
    whole = pl.BlockSpec(memory_space=pltpu.VMEM)
    cells = rows * cols
    return pl.pallas_call(
        ocean_kernel_body,
        out_shape=jax.ShapeDtypeStruct((rows, cols, width), jnp.bfloat16),
        in_specs=[whole] * 5 + [pl.BlockSpec(memory_space=pl.ANY)],
        out_specs=whole,
        scratch_shapes=[
            pltpu.VMEM(field.shape, jnp.float32),
            pltpu.VMEM((2 * cols, width), jnp.float32),
        ],
        compiler_params=pltpu.CompilerParams(vmem_limit_bytes=32 * 1024 * 1024),
        cost_estimate=pl.CostEstimate(
            flops=4 * cells * width * hidden + 98 * cells * width * 64,
            bytes_accessed=4 * field.size + 4 * up_weight.size,
            transcendentals=cells * hidden,
        ),
    )(field, taps, gain[None, :], up_weight, down_weight, after)


def local(
    atm_state,
    ocean_state,
    wet_mask,
    legendre,
    quad_weight,
    spec_real,
    spec_imag,
    degree_gain,
    atm_gain,
    atm_up,
    atm_down,
    atm_to_surface,
    surface_to_atm,
    ocean_to_surface,
    surface_to_ocean,
    ocean_kernel,
    ocean_gain,
    ocean_up,
    ocean_down,
):
    col_count = lax.axis_size(COLUMNS)
    lat_dev, lon_dev, _ = atm_state.shape
    circle = lon_dev * col_count
    wet = wet_mask.astype(jnp.float32)[:, :, None]
    ocean_flux = (
        jnp.dot(ocean_state, ocean_to_surface, preferred_element_type=jnp.float32) * wet
    ).astype(jnp.bfloat16)
    atm_flux = jnp.dot(atm_state, atm_to_surface, preferred_element_type=jnp.float32).astype(
        jnp.bfloat16
    )
    flux_here = lax.all_to_all(ocean_flux, "comp", split_axis=1, concat_axis=0, tiled=True)
    flux_sea = lax.all_to_all(atm_flux, "comp", split_axis=0, concat_axis=1, tiled=True)
    forced = atm_state.astype(jnp.float32) + jnp.dot(
        flux_here, surface_to_atm, preferred_element_type=jnp.float32
    )
    normed = layer_norm(forced, atm_gain[0]).astype(jnp.bfloat16)
    run_spectral = (
        folded_spectral
        if folds(circle, lat_dev, col_count, lax.axis_size(EVERY))
        else plain_spectral
    )
    spectral, stages = run_spectral(
        normed, legendre, quad_weight, spec_real, spec_imag, degree_gain, circle
    )
    mixed = forced + spectral.astype(jnp.float32)
    normed_two = layer_norm(mixed, atm_gain[1]).astype(jnp.bfloat16)
    hidden = jax.nn.gelu(jnp.dot(normed_two, atm_up, preferred_element_type=jnp.float32)).astype(
        jnp.bfloat16
    )
    atm_out = (mixed + jnp.dot(hidden, atm_down, preferred_element_type=jnp.float32)).astype(
        jnp.bfloat16
    )
    ocean_in = (
        ocean_state.astype(jnp.float32)
        + wet * jnp.dot(flux_sea, surface_to_ocean, preferred_element_type=jnp.float32)
    ).astype(jnp.bfloat16)
    stencil_reach = STENCIL_TAPS // 2 * OCEAN_DILATION
    sides = ((("lat", "comp"), 0), ("lon", 1))
    current = ocean_in
    quick = ocean_in.shape[0] % (2 * OCEAN_DILATION) == 0 and ocean_in.shape[2] % 128 == 0
    for k in range(2):
        field = padded(current, sides, stencil_reach)
        weights = (ocean_kernel[k], ocean_gain[k], ocean_up[k], ocean_down[k])
        if quick:
            current = fast_ocean_block(field, *weights, stages[k])
        else:
            current = ocean_block(field, *weights)
    ocean_out = jnp.where(wet_mask[:, :, None] == 1, current, ocean_state)
    return (atm_out, ocean_out)


def solution(mesh):
    placed = (
        P("lat", ("lon", "comp"), None),
        P(("lat", "comp"), "lon", None),
        P(("lat", "comp"), "lon"),
        P(("lat", "lon", "comp"), None, None),
        P(),
        P(),
        P(),
        P(),
        P(),
        P(),
        P(),
        P(),
        P(),
        P(),
        P(),
        P(),
        P(),
        P(),
        P(),
    )

    return jax.shard_map(
        local,
        mesh=mesh,
        in_specs=placed,
        out_specs=(P("lat", ("lon", "comp"), None), P(("lat", "comp"), "lon", None)),
        check_vma=False,
    )
```
